32 devices in a mesh: ctx: 8 (over z, x), hd: 4 (over y, core).
Axes of the slice: x: 2, y: 2, z: 4, core: 2. Of those that a mesh axis runs over, the one named last changes fastest.
Arguments:
- queries: bfloat16 [4096, 3584], P(('ctx', 'hd')), may hold values from -8 to 8
- keys: bfloat16 [4096, 512], P(('ctx', 'hd')), may hold values from -8 to 8
- values: bfloat16 [4096, 512], P(('ctx', 'hd')), may hold values from -6 to 6
- window_blocks: int32 [32], replicated, may hold values from 1 to 16, as said below
- far_use: int32 [32, 4], replicated, may hold values from 0 to 1, as said below
Outputs:
- attended: bfloat16 [4096, 3584], P(('ctx', 'hd'))
The draws below stay inside these ranges and needn't reach their ends.
Inputs may be any that keep to these rules, and one draw needn't show every extreme that they name: `window_blocks`: the value 16 occurs in every draw. far_use[b, e] is 0 wherever b < 16 * 2^e.
All inputs are finite; a program needn't handle non-finite values.
Results may differ from the reference program's by a relative error of at most 0.004.
Values may be sent and summed in bfloat16 or wider, within the bound.
A program may use at most 64 MiB of HBM per device.

```python
import jax
import jax.numpy as jnp
from jax import lax

QUERY_HEADS = 28
KEY_VALUE_HEADS = 4
HEAD_SIZE = 128
BLOCK_TOKENS = 128
WIN = 16
NPOW = 4
SEQUENCE_TOKENS = 4096
NBLK = 32


def draw_queries(key, part):
    simple_sample = jnp.clip(2.0 * jax.random.normal(jax.random.fold_in(key, 31), (SEQUENCE_TOKENS, QUERY_HEADS, HEAD_SIZE), jnp.float32), -8.0, 8.0)
    return simple_sample.reshape(SEQUENCE_TOKENS, QUERY_HEADS * HEAD_SIZE).astype(jnp.bfloat16)


def draw_keys(key, part):
    simple_sample = jnp.clip(jax.random.normal(jax.random.fold_in(key, 37), (SEQUENCE_TOKENS, KEY_VALUE_HEADS, HEAD_SIZE), jnp.float32), -8.0, 8.0)
    return simple_sample.reshape(SEQUENCE_TOKENS, KEY_VALUE_HEADS * HEAD_SIZE).astype(jnp.bfloat16)


def draw_window_blocks(key, part):
    base_key = jax.random.fold_in(key, 41)
    full_width = jax.random.randint(jax.random.fold_in(base_key, 1), (NBLK,), 0, 4) == 0
    short_width = jax.random.randint(jax.random.fold_in(base_key, 2), (NBLK,), 1, WIN // 4 + 1)
    widths = jnp.where(full_width, WIN, short_width)
    forced = jax.random.randint(jax.random.fold_in(base_key, 3), (), 0, NBLK)
    return jnp.where(jnp.arange(NBLK) == forced, WIN, widths).astype(jnp.int32)


def draw_far_use(key, part):
    base_key = jax.random.fold_in(key, 43)
    coin_flips = jax.random.randint(base_key, (NBLK, NPOW), 0, 2)
    reach_blocks = WIN * 2 ** jnp.arange(NPOW, dtype=jnp.int32)
    live = jnp.arange(NBLK, dtype=jnp.int32)[:, None] >= reach_blocks[None, :]
    return jnp.where(live, coin_flips, 0).astype(jnp.int32)


def level_of(own_key, shape, cuts, low, largest):
    def one(dim, blocks):
        heights = jax.random.uniform(jax.random.fold_in(jax.random.fold_in(own_key, 6), dim), (blocks,), jnp.float32, low / len(cuts), largest / len(cuts))
        return jnp.repeat(jnp.exp(heights), shape[dim] // blocks).reshape((-1,) + (1,) * (len(shape) - dim - 1))

    gain = one(*cuts[0])
    for cut in cuts[1:]:
        gain = gain * one(*cut)
    return gain


def gaussian(rng, dims, scale, bound, shards=(), kind=jnp.bfloat16):
    drawn = jax.random.normal(rng, dims, jnp.float32) * scale
    if len(shards) > 0:
        drawn = level_of(rng, dims, shards, -0.22, 0.18) * drawn
    return jnp.clip(drawn, min=-bound, max=bound).astype(kind)


def setup_inputs(seed: int = 0) -> dict:
    streams_of = jax.random.split(jax.random.key(seed), 6)
    queries = draw_queries(jax.random.fold_in(streams_of[5], 71), 0)
    keys = draw_keys(jax.random.fold_in(streams_of[5], 71), 0)
    values = gaussian(streams_of[2], (SEQUENCE_TOKENS, KEY_VALUE_HEADS * HEAD_SIZE), 1.0, 6.0, ((0, 32),))
    window_blocks = draw_window_blocks(jax.random.fold_in(streams_of[5], 71), 0)
    far_use = draw_far_use(jax.random.fold_in(streams_of[5], 71), 0)
    return dict(queries=queries, keys=keys, values=values, window_blocks=window_blocks, far_use=far_use)


def reference(queries, keys, values, window_blocks, far_use):
    group_width = QUERY_HEADS // KEY_VALUE_HEADS
    score_scale = HEAD_SIZE ** -0.5
    padding_rows = WIN * BLOCK_TOKENS
    heads_of_keys = keys.reshape(SEQUENCE_TOKENS, KEY_VALUE_HEADS, HEAD_SIZE)
    heads_of_values = values.reshape(SEQUENCE_TOKENS, KEY_VALUE_HEADS, HEAD_SIZE)
    padded_keys = jnp.concatenate([jnp.zeros((padding_rows, KEY_VALUE_HEADS, HEAD_SIZE), keys.dtype), heads_of_keys])
    padded_values = jnp.concatenate([jnp.zeros((padding_rows, KEY_VALUE_HEADS, HEAD_SIZE), values.dtype), heads_of_values])
    slot_index = jnp.arange(WIN * BLOCK_TOKENS, dtype=jnp.int32)
    slot_distance = WIN - 1 - slot_index // BLOCK_TOKENS
    slot_inside = slot_index % BLOCK_TOKENS
    row_token = jnp.arange(BLOCK_TOKENS, dtype=jnp.int32)

    def one_block(block_number):
        block_of_queries = lax.dynamic_slice_in_dim(queries, block_number * BLOCK_TOKENS, BLOCK_TOKENS, 0).reshape(BLOCK_TOKENS, KEY_VALUE_HEADS, group_width, HEAD_SIZE)
        win_keys = lax.dynamic_slice_in_dim(padded_keys, (block_number + 1) * BLOCK_TOKENS, WIN * BLOCK_TOKENS, 0)
        win_values = lax.dynamic_slice_in_dim(padded_values, (block_number + 1) * BLOCK_TOKENS, WIN * BLOCK_TOKENS, 0)
        key_parts = [win_keys]
        value_parts = [win_values]
        for exponent in range(NPOW):
            far_start = (jnp.maximum(block_number - WIN * 2 ** exponent, 0) * BLOCK_TOKENS).astype(jnp.int32)
            key_parts.append(lax.dynamic_slice_in_dim(heads_of_keys, far_start, BLOCK_TOKENS, 0))
            value_parts.append(lax.dynamic_slice_in_dim(heads_of_values, far_start, BLOCK_TOKENS, 0))
        all_keys = jnp.concatenate(key_parts)
        all_values = jnp.concatenate(value_parts)
        win_ok = (slot_distance < window_blocks[block_number]) & (block_number - slot_distance >= 0)
        win_ok = win_ok[None, :] & ((slot_distance > 0)[None, :] | (slot_inside[None, :] <= row_token[:, None]))
        far_ok = jnp.repeat(far_use[block_number] == 1, BLOCK_TOKENS)
        allowed = jnp.concatenate([win_ok, jnp.broadcast_to(far_ok[None, :], (BLOCK_TOKENS, NPOW * BLOCK_TOKENS))], axis=1)
        scores = jnp.einsum('tkgd,skd->kgts', block_of_queries.astype(jnp.float32), all_keys.astype(jnp.float32)) * score_scale
        scores = jnp.where(allowed[None, None], scores, -jnp.inf)
        row_top = jnp.max(scores, axis=-1, keepdims=True)
        exponentials = jnp.exp(scores - row_top)
        weights = exponentials.astype(jnp.bfloat16)
        row_total = jnp.sum(exponentials, axis=-1, keepdims=True)
        summed = jnp.einsum('kgts,skd->tkgd', weights.astype(jnp.float32), all_values.astype(jnp.float32))
        result = summed / jnp.transpose(row_total, (2, 0, 1, 3))
        return result.reshape(BLOCK_TOKENS, QUERY_HEADS * HEAD_SIZE).astype(jnp.bfloat16)

    blocks_out = lax.map(one_block, jnp.arange(NBLK, dtype=jnp.int32))
    return blocks_out.reshape(SEQUENCE_TOKENS, QUERY_HEADS * HEAD_SIZE)
```

```python
import functools
import math

import jax
import jax.numpy as jnp
from jax import lax
from jax.experimental import pallas as pl
from jax.experimental.pallas import tpu as pltpu
from jax.sharding import PartitionSpec as P

QUERY_HEADS = 28
KEY_VALUE_HEADS = 4
HEAD_SIZE = 128
BLOCK_TOKENS = 128
WIN = 16
NPOW = 4
GROUP = QUERY_HEADS // KEY_VALUE_HEADS
NEG = -1e30
EXP_SCALE = HEAD_SIZE ** (-0.5) * math.log2(math.e)

PLANE = 4
UNITS = WIN // 2 + 1


def kernel(sizes, wb_ref, far_ref, q_hbm, k_hbm, v_hbm, o_ref,
           q_ref, kv, top, total, accum, local_sem, send_sem, recv_sem, pair_send, pair_recv):
    ctx_size, hd_size = sizes
    devices = ctx_size * hd_size
    pairs = devices // 2
    far_steps = [WIN // 2 * 2**e for e in range(1, NPOW) if WIN // 2 * 2**e < pairs]
    me = lax.axis_index("ctx") * hd_size + lax.axis_index("hd")
    pair = me // 2
    core = me % 2
    place = pair % PLANE
    partner = me + 1 - 2 * core

    def at(device):
        return (device // hd_size, device % hd_size)

    def local(group):
        cols = pl.ds(pl.multiple_of(group * HEAD_SIZE, HEAD_SIZE), HEAD_SIZE)
        return [pltpu.make_async_copy(ref.at[:, cols], kv.at[0, group, core, i],
                                      local_sem.at[group, i])
                for i, ref in enumerate((k_hbm, v_hbm))]

    load = pltpu.make_async_copy(q_hbm, q_ref, local_sem.at[KEY_VALUE_HEADS, 0])
    for group in range(KEY_VALUE_HEADS):
        for copy in local(group):
            copy.start()
    load.start()

    barrier = pltpu.get_barrier_semaphore()
    along_x = 2 - 4 * (place // 2)
    along_y = 1 - 2 * (place % 2)
    steps = [PLANE] + far_steps

    def greet(device):
        pl.semaphore_signal(barrier, inc=1, device_id=at(device),
                            device_id_type=pl.DeviceIdType.MESH)

    greet(partner)
    for delta in (along_x, along_y):
        greet(me + 2 * delta)
    for d in steps:
        @pl.when(pair + d < pairs)
        def _(d=d):
            greet(me + 2 * d)

        @pl.when(pair >= d)
        def _(d=d):
            greet(me - 2 * d)
    peers = jnp.int32(3)
    for d in steps:
        peers = peers + jnp.where(pair + d < pairs, 1, 0) + jnp.where(pair >= d, 1, 0)
    pl.semaphore_wait(barrier, peers)

    deltas = (PLANE, along_x, along_y)

    def send(direction, slot, group, target=None):
        delta = deltas[direction] if direction < 3 else far_steps[direction - 3]
        target = slot + delta if target is None else target
        return pltpu.make_async_remote_copy(
            src_ref=kv.at[slot, group, core], dst_ref=kv.at[target, group, core],
            send_sem=send_sem.at[direction, slot], recv_sem=recv_sem.at[target, group],
            device_id=at(me + 2 * delta), device_id_type=pl.DeviceIdType.MESH)

    def sent(direction, slot):
        pltpu.make_async_remote_copy(
            src_ref=kv.at[slot, :, core], dst_ref=kv.at[slot, :, core],
            send_sem=send_sem.at[direction, slot], recv_sem=recv_sem.at[slot, 0],
            device_id=at(partner), device_id_type=pl.DeviceIdType.MESH).wait_send()

    def arrived(slot, group):
        pltpu.make_async_remote_copy(
            src_ref=kv.at[slot, group, core], dst_ref=kv.at[slot, group, core],
            send_sem=send_sem.at[0, slot], recv_sem=recv_sem.at[slot, group],
            device_id=at(partner), device_id_type=pl.DeviceIdType.MESH).wait_recv()

    def hand(slot, group):
        return pltpu.make_async_remote_copy(
            src_ref=kv.at[slot, group, core], dst_ref=kv.at[slot, group, core],
            send_sem=pair_send.at[slot], recv_sem=pair_recv.at[slot, group],
            device_id=at(partner), device_id_type=pl.DeviceIdType.MESH)

    def given(slot):
        pltpu.make_async_remote_copy(
            src_ref=kv.at[slot, :, core], dst_ref=kv.at[slot, :, core],
            send_sem=pair_send.at[slot], recv_sem=pair_recv.at[slot, 0],
            device_id=at(partner), device_id_type=pl.DeviceIdType.MESH).wait_send()

    def handed(slot, group):
        pltpu.make_async_remote_copy(
            src_ref=kv.at[slot, group, 1 - core], dst_ref=kv.at[slot, group, 1 - core],
            send_sem=pair_send.at[slot], recv_sem=pair_recv.at[slot, group],
            device_id=at(partner), device_id_type=pl.DeviceIdType.MESH).wait_recv()

    UP, X, Y = 0, 1, 2
    above = pair + PLANE < pairs
    own = [(UP, above), (X, along_x > 0), (Y, along_y > 0)]
    own += [(3 + i, pair + d < pairs) for i, d in enumerate(far_steps)]

    for group in range(KEY_VALUE_HEADS):
        for copy in local(group):
            copy.wait()
        for direction, cond in own[:3]:
            @pl.when(cond)
            def _(direction=direction, group=group):
                send(direction, 0, group).start()
        hand(0, group).start()
    for i in range(len(far_steps)):
        @pl.when(own[3 + i][1])
        def _(i=i):
            for group in range(KEY_VALUE_HEADS):
                send(3 + i, 0, group, UNITS + i).start()

    window = wb_ref[me]

    def pick(*values):
        out = jnp.int32(values[-1])
        for i in range(PLANE - 1):
            out = jnp.where(place == i, values[i], out)
        return out

    high = place >= 2
    odd = place % 2 == 1
    stage = [
        [(PLANE, [(UP, above), (X, None), (Y, None)]), (2, [(Y, high)])],
        [(pick(3, 1, 1, 1), [(X, place == 0)]), (2 * PLANE, [(X, high), (Y, odd)])],
        [(6, [(Y, jnp.logical_not(high))]), (pick(7, 5, 3, 5), [(X, place > 0)])],
        [(2 * place + 1, []), (pick(5, 7, 7, 3), [])],
    ]

    def handle(number, group):
        for slot, forwards in stage[number]:
            @pl.when(pair >= slot)
            def _(slot=slot, forwards=forwards):
                arrived(slot, group)
                for direction, cond in forwards:
                    if cond is None:
                        send(direction, slot, group).start()
                    else:
                        @pl.when(cond)
                        def _(direction=direction):
                            send(direction, slot, group).start()
                hand(slot, group).start()

    def update(units, group, mask):
        rows = 2 * BLOCK_TOKENS

        def gather(which):
            return jnp.concatenate(
                [kv[u, group, :, which].reshape(rows, HEAD_SIZE) for u in units], axis=0)

        keys = gather(0)
        vals = gather(1)
        scores = []
        for j in range(GROUP):
            head = group * GROUP + j
            q = q_ref[:, pl.ds(pl.multiple_of(head * HEAD_SIZE, HEAD_SIZE), HEAD_SIZE)]
            scores.append(lax.dot_general(q, keys, (((1,), (1,)), ((), ())),
                                          preferred_element_type=jnp.float32))
        weights = []
        factors = []
        for j in range(GROUP):
            head = group * GROUP + j
            s = mask(scores[j])
            parts = [s[:, i:i + BLOCK_TOKENS] for i in range(0, s.shape[1], BLOCK_TOKENS)]
            peak = jnp.max(functools.reduce(jnp.maximum, parts), axis=-1, keepdims=True)
            before = top[head]
            now = jnp.maximum(before, peak)
            factor = jnp.exp2((before - now) * EXP_SCALE)
            exps = [jnp.exp2((part - now) * EXP_SCALE) for part in parts]
            weights.append(jnp.concatenate([p.astype(jnp.bfloat16) for p in exps], axis=1))
            factors.append(factor)
            top[head] = now
            total[head] = total[head] * factor + functools.reduce(jnp.add, exps)
        for j in range(GROUP):
            head = group * GROUP + j
            accum[head] = accum[head] * factors[j] + jnp.dot(
                weights[j], vals, preferred_element_type=jnp.float32)

    top[...] = jnp.full_like(top, NEG)
    total[...] = jnp.zeros_like(total)
    accum[...] = jnp.zeros_like(accum)

    @pl.loop(1, UNITS)
    def _(unit):
        @pl.when(pair < unit)
        def _():
            kv[unit] = jnp.zeros(kv.shape[1:], kv.dtype)

    load.wait()

    row = lax.broadcasted_iota(jnp.int32, (BLOCK_TOKENS, 2 * BLOCK_TOKENS), 0)
    col = lax.broadcasted_iota(jnp.int32, (BLOCK_TOKENS, 2 * BLOCK_TOKENS), 1)
    edge = row + core * BLOCK_TOKENS
    floor = jnp.where(window > 1, 0, core * BLOCK_TOKENS)
    causal = (col <= edge) & (col >= floor)

    @pl.loop(0, KEY_VALUE_HEADS)
    def _(group):
        handed(0, group)
        update((0,), group, lambda s: jnp.where(causal, s, NEG))
        handle(0, group)

    def absorb(parts, group):
        bias = []
        for _, d, reach, flag in parts:
            for i in range(2):
                j = 2 * d + core - i
                ok = (pair >= d) & ((j < window) | ((j == reach) & (flag == 1)))
                bias.append(jnp.full((1, BLOCK_TOKENS), jnp.where(ok, 0.0, NEG), jnp.float32))
        bias = jnp.concatenate(bias, axis=1)
        update([part[0] for part in parts], group, lambda s: s + bias)

    flag = far_ref[0, me]

    for number in range(len(stage)):
        slots = [slot for slot, _ in stage[number]]

        @pl.loop(0, KEY_VALUE_HEADS)
        def _(group, number=number, slots=slots):
            @pl.when(pair >= functools.reduce(jnp.minimum, slots))
            def _():
                for slot in slots:
                    @pl.when(pair >= slot)
                    def _(slot=slot):
                        handed(slot, group)
                absorb([(slot, slot, WIN, flag) for slot in slots], group)

            if number + 1 < len(stage):
                handle(number + 1, group)

    for i, d in enumerate(far_steps):
        @pl.when(pair >= d)
        def _(i=i, d=d):
            @pl.loop(0, KEY_VALUE_HEADS)
            def _(group):
                arrived(UNITS + i, group)
                hand(UNITS + i, group).start()
                handed(UNITS + i, group)
                absorb([(UNITS + i, d, 2 * d, far_ref[i + 1, me])], group)

    @pl.loop(0, KEY_VALUE_HEADS)
    def _(group):
        for j in range(GROUP):
            head = group * GROUP + j
            whole_total = jnp.sum(total[head], axis=-1, keepdims=True)
            o_ref[:, pl.ds(pl.multiple_of(head * HEAD_SIZE, HEAD_SIZE), HEAD_SIZE)] = (
                accum[head] / whole_total).astype(o_ref.dtype)

    for direction, cond in own:
        @pl.when(cond)
        def _(direction=direction):
            sent(direction, 0)
    given(0)
    for step in stage:
        for slot, forwards in step:
            @pl.when(pair >= slot)
            def _(slot=slot, forwards=forwards):
                for direction, cond in forwards:
                    if cond is None:
                        sent(direction, slot)
                    else:
                        @pl.when(cond)
                        def _(direction=direction):
                            sent(direction, slot)
                given(slot)
    for i, d in enumerate(far_steps):
        @pl.when(pair >= d)
        def _(i=i):
            given(UNITS + i)


def per_device(sizes, queries, keys, values, window_blocks, far_use):
    tokens, kv_width = keys.shape
    assert tokens == BLOCK_TOKENS
    pairs = sizes[0] * sizes[1] // 2
    fars = len([e for e in range(1, NPOW) if WIN // 2 * 2**e < pairs])
    units = UNITS + fars
    vmem = pl.BlockSpec(memory_space=pltpu.VMEM)
    hbm = pl.BlockSpec(memory_space=pl.ANY)
    smem = pl.BlockSpec(memory_space=pltpu.SMEM)
    state = (QUERY_HEADS, BLOCK_TOKENS, HEAD_SIZE)
    return pl.pallas_call(
        functools.partial(kernel, sizes),
        out_shape=jax.ShapeDtypeStruct(queries.shape, queries.dtype),
        in_specs=[smem, smem, hbm, hbm, hbm],
        out_specs=vmem,
        scratch_shapes=[
            pltpu.VMEM(queries.shape, queries.dtype),
            pltpu.VMEM((units, KEY_VALUE_HEADS, 2, 2, tokens, HEAD_SIZE), keys.dtype),
            pltpu.VMEM(state, jnp.float32),
            pltpu.VMEM(state, jnp.float32),
            pltpu.VMEM(state, jnp.float32),
            pltpu.SemaphoreType.DMA((KEY_VALUE_HEADS + 1, 2)),
            pltpu.SemaphoreType.DMA((3 + fars, units)),
            pltpu.SemaphoreType.DMA((units, KEY_VALUE_HEADS)),
            pltpu.SemaphoreType.DMA((units,)),
            pltpu.SemaphoreType.DMA((units, KEY_VALUE_HEADS)),
        ],
        compiler_params=pltpu.CompilerParams(
            collective_id=0, has_side_effects=True, vmem_limit_bytes=63 * 2**20),
    )(window_blocks, far_use.T, queries, keys, values)


def solution(mesh):
    placed = (P(("ctx", "hd"), None), P(("ctx", "hd"), None), P(("ctx", "hd"), None), P(), P())
    sizes = (mesh.shape["ctx"], mesh.shape["hd"])
    return jax.shard_map(
        functools.partial(per_device, sizes), mesh=mesh, in_specs=placed,
        out_specs=P(("ctx", "hd"), None), check_vma=False
    )
```
